512 devices in a mesh: dp: 16 (over z_hi, x), seq: 32 (over y, z_lo, core).
Axes of the slice: x: 4, y: 8, z: 8 (z_hi: 4, z_lo: 2; z = z_hi * 2 + z_lo), core: 2. Of those that a mesh axis runs over, the one named last changes fastest.
Arguments:
- frame_features: bfloat16 [32, 4, 64, 32, 512], P('dp', None, 'seq'), may hold values from -6 to 6
- conv_weight: bfloat16 [27, 512, 32], replicated, may hold values from -0.0546875 to 0.0546875
- conv_bias: float32 [32], replicated, may hold values from -0.5 to 0.5
- vae_noise: float32 [32, 2048, 64], P('dp', 'seq'), may hold values from -6 to 6
- flow_noise: float32 [32, 2048, 64], P('dp', 'seq'), may hold values from -6 to 6
- head_queries: bfloat16 [32, 2048, 2048], P('dp', 'seq'), may hold values from -48 to 48
- head_keys: bfloat16 [32, 2048, 2048], P('dp', 'seq'), may hold values from -48 to 48
- head_values: bfloat16 [32, 2048, 2048], P('dp', 'seq'), may hold values from -6 to 6
- out_weight: bfloat16 [2048, 64], replicated, may hold values from -0.125 to 0.125
- out_bias: float32 [64], replicated, may hold values from -1 to 1
Outputs:
- grad_queries: bfloat16 [32, 2048, 2048], P('dp', 'seq')
- grad_keys: bfloat16 [32, 2048, 2048], P('dp', 'seq')
- grad_values: bfloat16 [32, 2048, 2048], P('dp', 'seq')
- grad_out_weight: float32 [2048, 64], P('seq')
The draws below stay inside these ranges and needn't reach their ends.
All inputs are finite; a program needn't handle non-finite values.
Results may differ from the reference program's by a relative error of at most 0.019.
Values may be sent and summed in bfloat16 or wider, within the bound.
No kernel may reach another device: no remote copies, remote signals or barrier semaphores. Data moves between devices by JAX's collectives and lax.ppermute only.
A program may use at most 64 MiB of HBM per device.

```python
import math
import jax
import jax.numpy as jnp
from jax import lax

HEADS = 16
HDIM = 128
CH = 512
LATC = 16
FRAMES = 4
LCOLS = 32
OUTW = 2048
PF = 64
LROWS = 64
SEQ_LEN = 2048
CLIPS = 32


def query_key_pair(key):
    base_key = jax.random.fold_in(key, 7301)
    query_seed, key_seed = jax.random.split(base_key, 2)
    full_shape = (CLIPS, SEQ_LEN, HEADS, HDIM)
    query_vals = jnp.clip(jax.random.normal(query_seed, full_shape, jnp.float32), -6.0, 6.0)
    key_vals = jnp.clip(jax.random.normal(key_seed, full_shape, jnp.float32), -6.0, 6.0)
    return (query_vals.reshape(CLIPS, SEQ_LEN, HEADS * HDIM), key_vals.reshape(CLIPS, SEQ_LEN, HEADS * HDIM))


def draw_head_queries(key, part):
    return query_key_pair(key)[0].astype(jnp.bfloat16)


def draw_head_keys(key, part):
    return query_key_pair(key)[1].astype(jnp.bfloat16)


def levels(key, extent, pieces, least, high):
    level, own = 1.0, jax.random.fold_in(key, 6)
    for axis_at, blocks in pieces:
        heights = jnp.exp(jax.random.uniform(jax.random.fold_in(own, axis_at), (blocks,), jnp.float32, least / len(pieces), high / len(pieces)))
        level = level * jnp.repeat(heights, extent[axis_at] // blocks).reshape([-1 if axis == axis_at else 1 for axis in range(len(extent))])
    return level


def scatter_about(rng, extent, spread, reach, cuts=(), kind=jnp.bfloat16):
    entries = spread * jax.random.normal(rng, extent, jnp.float32)
    if cuts:
        entries = entries * levels(rng, extent, cuts, -0.22, 0.18)
    return jnp.clip(entries, -reach, reach).astype(kind)


def setup_inputs(seed: int = 0) -> dict:
    key_of = jax.random.split(jax.random.key(seed), 11)
    frame_features = scatter_about(key_of[0], (CLIPS, FRAMES, LROWS, LCOLS, CH), 1.0, 6.0, ((0, 16), (2, 32)))
    conv_weight = scatter_about(key_of[1], (27, CH, 2 * LATC), (27 * CH) ** -0.5, 0.0546875)
    conv_bias = jnp.clip(jax.random.uniform(key_of[2], (2 * LATC,), jnp.float32, -0.5, 0.5), -0.5, 0.5)
    vae_noise = scatter_about(key_of[3], (CLIPS, SEQ_LEN, PF), 1.0, 6.0, ((0, 16), (1, 32)), jnp.float32)
    flow_noise = scatter_about(key_of[4], (CLIPS, SEQ_LEN, PF), 1.0, 6.0, ((0, 16), (1, 32)), jnp.float32)
    head_queries = draw_head_queries(jax.random.fold_in(key_of[10], 71), 0)
    head_keys = draw_head_keys(jax.random.fold_in(key_of[10], 71), 0)
    head_values = scatter_about(key_of[7], (CLIPS, SEQ_LEN, OUTW), 1.0, 6.0, ((0, 16), (1, 32)))
    out_weight = scatter_about(key_of[8], (OUTW, PF), OUTW ** -0.5, 0.125)
    out_bias = jnp.clip(jax.random.uniform(key_of[9], (PF,), jnp.float32, -1.0, 1.0), -1.0, 1.0)
    return dict(frame_features=frame_features, conv_weight=conv_weight, conv_bias=conv_bias, vae_noise=vae_noise, flow_noise=flow_noise, head_queries=head_queries, head_keys=head_keys, head_values=head_values, out_weight=out_weight, out_bias=out_bias)


latent_factor = 0.476986

def causal_conv(padded_rows, conv_weight, conv_bias):
    clip_count, frame_count, padded_height, column_count, channels = padded_rows.shape
    row_count = padded_height - 2
    opening = padded_rows[:, :1]
    timed = jnp.concatenate([opening, opening, padded_rows], axis=1)
    border = jnp.zeros((clip_count, frame_count + 2, padded_height, 1, channels), padded_rows.dtype)
    framed = jnp.concatenate([border, timed, border], axis=3)
    out_channels = conv_weight.shape[2]
    summed = jnp.zeros((clip_count * frame_count * row_count * column_count, out_channels), jnp.float32)
    for frame_tap in range(3):
        for row_tap in range(3):
            for column_tap in range(3):
                window = framed[:, frame_tap:frame_tap + frame_count, row_tap:row_tap + row_count, column_tap:column_tap + column_count]
                summed = summed + jnp.dot(window.reshape(-1, channels), conv_weight[frame_tap * 9 + row_tap * 3 + column_tap], preferred_element_type=jnp.float32)
    summed = summed + conv_bias
    return summed.reshape(clip_count, frame_count, row_count, column_count, out_channels)

def to_tokens(grid):
    clip_count, frame_count, row_count, column_count, channels = grid.shape
    shaped = grid.reshape(clip_count, frame_count, row_count // 2, 2, column_count // 2, 2, channels)
    shaped = shaped.transpose(0, 2, 1, 4, 6, 3, 5)
    return shaped.reshape(clip_count, row_count // 2 * frame_count * (column_count // 2), channels * 4)

def make_target(encoded, vae_noise, flow_noise):
    mean_tokens = to_tokens(encoded[..., :LATC])
    logvar_tokens = to_tokens(encoded[..., LATC:])
    latent = mean_tokens + jnp.exp(0.5 * logvar_tokens) * vae_noise
    return flow_noise - latent_factor * latent

def clip_backward(query_rows, key_rows, value_rows, target, out_weight, out_bias):
    length = query_rows.shape[0]
    score_scale = 1.0 / math.sqrt(HDIM)
    query_heads = query_rows.reshape(length, HEADS, HDIM).astype(jnp.float32)
    key_heads = key_rows.reshape(length, HEADS, HDIM).astype(jnp.float32)
    value_heads = value_rows.reshape(length, HEADS, HDIM).astype(jnp.float32)
    scores = jnp.einsum('qhd,khd->hqk', query_heads, key_heads) * score_scale
    shifted = jnp.exp(scores - lax.optimization_barrier(jnp.max(scores, axis=-1, keepdims=True)))
    attn_probs = lax.optimization_barrier((shifted / lax.optimization_barrier(jnp.sum(shifted, axis=-1, keepdims=True))).astype(jnp.bfloat16))
    probs_wide = attn_probs.astype(jnp.float32)
    attended = jnp.einsum('hqk,khd->qhd', probs_wide, value_heads).astype(jnp.bfloat16).reshape(length, OUTW)
    attended = lax.optimization_barrier(attended)
    predicted = jnp.dot(attended, out_weight, preferred_element_type=jnp.float32) + out_bias
    errors = lax.optimization_barrier((predicted - target).astype(jnp.bfloat16))
    grad_attended = jnp.dot(errors, out_weight.T, preferred_element_type=jnp.float32).astype(jnp.bfloat16)
    grad_attended = lax.optimization_barrier(grad_attended)
    weight_part = jnp.dot(attended.T, errors, preferred_element_type=jnp.float32)
    grad_heads = grad_attended.reshape(length, HEADS, HDIM).astype(jnp.float32)
    attended_heads = attended.reshape(length, HEADS, HDIM).astype(jnp.float32)
    grad_probs = jnp.einsum('qhd,khd->hqk', grad_heads, value_heads)
    row_dots = lax.optimization_barrier(jnp.sum(grad_heads * attended_heads, axis=-1))
    grad_scores = (probs_wide * (grad_probs - row_dots.T[:, :, None])).astype(jnp.bfloat16)
    grad_scores = lax.optimization_barrier(grad_scores).astype(jnp.float32)
    grad_queries = (jnp.einsum('hqk,khd->qhd', grad_scores, key_heads) * score_scale).astype(jnp.bfloat16)
    grad_keys = (jnp.einsum('hqk,qhd->khd', grad_scores, query_heads) * score_scale).astype(jnp.bfloat16)
    grad_values = jnp.einsum('hqk,qhd->khd', probs_wide, grad_heads).astype(jnp.bfloat16)
    return (grad_queries.reshape(length, OUTW), grad_keys.reshape(length, OUTW), grad_values.reshape(length, OUTW), weight_part)

def reference(frame_features, conv_weight, conv_bias, vae_noise, flow_noise, head_queries, head_keys, head_values, out_weight, out_bias):

    def one_clip(clip_items):
        features, noise_vae, noise_flow, query_rows, key_rows, value_rows = clip_items
        activated = lax.optimization_barrier(jax.nn.silu(features.astype(jnp.float32)).astype(jnp.bfloat16))
        padded = jnp.pad(activated, ((0, 0), (1, 1), (0, 0), (0, 0)))
        encoded = causal_conv(padded[None], conv_weight, conv_bias)
        target = make_target(encoded, noise_vae[None], noise_flow[None])[0]
        return clip_backward(query_rows, key_rows, value_rows, target, out_weight, out_bias)
    grad_queries, grad_keys, grad_values, weight_parts = lax.map(one_clip, (frame_features, vae_noise, flow_noise, head_queries, head_keys, head_values))
    return (grad_queries, grad_keys, grad_values, lax.optimization_barrier(jnp.sum(weight_parts, axis=0)))
```

```python
import math

import jax
import jax.numpy as jnp
from jax import lax
from jax.experimental import pallas as pl
from jax.experimental.pallas import tpu as pltpu
from jax.sharding import PartitionSpec as P

HEADS = 16
HDIM = 128
LATC = 16
RANKS = 32
TOK = 64
HALF = TOK // 2
SEQ = RANKS * TOK
FEAT = 64
SCALE = 1.0 / math.sqrt(HDIM)
EXP2_SCALE = SCALE * math.log2(math.e)
ROWS = 256
PIECES = ROWS // TOK
STEPS = SEQ // ROWS
BACK_ROWS = 512
SUB_BACK = 256
BACK_PIECES = BACK_ROWS // TOK
BACK_STEPS = SEQ // BACK_ROWS
latent_factor = 0.476986

NT = (((1,), (1,)), ((), ()))
TN = (((0,), (0,)), ((), ()))
F32 = jnp.float32
BF16 = jnp.bfloat16


def mm(a, b, dims=(((1,), (0,)), ((), ()))):
    return lax.dot_general(a, b, dims, preferred_element_type=F32)


def pack_kernel(q_ref, k_ref, v_ref, out_ref):
    for part, ref in enumerate((q_ref, k_ref, v_ref)):
        for head in range(HEADS):
            out_ref[head, 0, part] = ref[0, :, head * HDIM : (head + 1) * HDIM]


def pack(q, k, v):
    spec = pl.BlockSpec((1, TOK, HEADS * HDIM), lambda c: (c, 0, 0))
    return pl.pallas_call(
        pack_kernel,
        grid=(2,),
        in_specs=[spec] * 3,
        out_specs=pl.BlockSpec((HEADS, 1, 3, TOK, HDIM), lambda c: (0, c, 0, 0, 0)),
        out_shape=jax.ShapeDtypeStruct((HEADS, 2, 3, TOK, HDIM), BF16),
        name="pack",
    )(q, k, v).reshape(RANKS, 3, TOK, HDIM)


def unpack_kernel(in_ref, q_ref, k_ref, v_ref, sems):
    for part, ref in enumerate((q_ref, k_ref, v_ref)):
        for clip in range(2):
            for head in range(HEADS):
                pltpu.make_async_copy(
                    in_ref.at[head, clip, part],
                    ref.at[clip, :, pl.ds(head * HDIM, HDIM)],
                    sems.at[part],
                ).start()
    for part, ref in enumerate((q_ref, k_ref, v_ref)):
        pltpu.make_async_copy(ref, ref, sems.at[part]).wait()


def unpack(back):
    shape = jax.ShapeDtypeStruct((2, TOK, HEADS * HDIM), BF16)
    return pl.pallas_call(
        unpack_kernel,
        in_specs=[pl.BlockSpec(memory_space=pltpu.VMEM)],
        out_specs=[pl.BlockSpec(memory_space=pltpu.HBM)] * 3,
        out_shape=[shape] * 3,
        scratch_shapes=[pltpu.SemaphoreType.DMA((3,))],
        compiler_params=pltpu.CompilerParams(vmem_limit_bytes=16 << 20),
        name="unpack",
    )(back.reshape(HEADS, 2, 3, TOK, HDIM))


def conv_kernel(x_ref, w_ref, own_ref, next_ref, prev_ref):
    x = x_ref[...].astype(F32)
    act = (x / (1.0 + jnp.exp(-x))).astype(BF16)
    lane = lax.broadcasted_iota(jnp.int32, (32, 512), 1)
    col = lane & 31
    row = (lane >> 5) & 1
    frame = (lane >> 6) & 3
    summed = []
    for dy in range(3):
        timed = []
        for dt in range(3):
            taps = mm(w_ref[pl.ds((9 * dt + 3 * dy) * 32, 96), :], act, NT)
            left = jnp.where(col == 0, 0.0, pltpu.roll(taps[0:32], 1, 1))
            right = jnp.where(col == 31, 0.0, pltpu.roll(taps[64:96], 511, 1))
            timed.append(taps[32:64] + left + right)
        z0, z1, z2 = timed
        one = jnp.where(frame == 0, z1, pltpu.roll(z1, 64, 1))
        two = jnp.where(
            frame == 0, z0, jnp.where(frame == 1, pltpu.roll(z0, 64, 1), pltpu.roll(z0, 128, 1))
        )
        summed.append(z2 + one + two)
    down, here, up = summed
    down_own = pltpu.roll(down, 32, 1)
    up_own = pltpu.roll(up, 480, 1)
    own_ref[...] = here + jnp.where(row == 1, down_own, up_own)
    next_ref[...] = jnp.where(row == 0, pltpu.roll(down, 480, 1), 0.0)
    prev_ref[...] = jnp.where(row == 1, pltpu.roll(up, 32, 1), 0.0)


def conv(features, weight):
    shape = jax.ShapeDtypeStruct((32, 512), F32)
    return pl.pallas_call(
        conv_kernel,
        out_shape=[shape] * 3,
        compiler_params=pltpu.CompilerParams(vmem_limit_bytes=32 << 20),
        cost_estimate=pl.CostEstimate(
            flops=2 * 512 * 512 * 864, bytes_accessed=2 << 20, transcendentals=1 << 18
        ),
        name="conv",
    )(features, weight)


def forward_kernel(
    got_ref, w_ref, p_out, a_out, r_out, pred_out, p_buf, a_buf, r_buf, pred_buf, sems
):
    k = got_ref[:, 1].reshape(SEQ, HDIM)
    v = got_ref[:, 2].reshape(SEQ, HDIM)
    copies = []

    def send(i, kind, buf, out, per):
        part = pl.ds(i * per, per)
        copies.append(pltpu.make_async_copy(buf.at[part], out.at[part], sems.at[kind, i]))
        copies[-1].start()

    def scored(i):
        return mm(got_ref[pl.ds(i * PIECES, PIECES), 0].reshape(ROWS, HDIM), k, NT)

    def softmaxed(i, scores):
        top = jnp.max(scores, axis=-1, keepdims=True)
        probs = jnp.exp2((scores - top) * EXP2_SCALE)
        inverse = 1.0 / jnp.sum(probs, axis=-1, keepdims=True)
        p_buf[pl.ds(i * ROWS, ROWS)] = probs.astype(BF16)
        return inverse

    def finished(i, inverse):
        rows = pl.ds(i * ROWS, ROWS)
        attended = (mm(p_buf[rows], v) * inverse).astype(BF16)
        r_buf[rows] = jnp.broadcast_to(inverse, (ROWS, HDIM))
        a_buf[rows] = attended
        pieces = attended.reshape(PIECES, 2, HALF, HDIM)
        pred = mm(pieces[:, 0].reshape(PIECES * HALF, HDIM), w_ref[0])
        pred = pred + mm(pieces[:, 1].reshape(PIECES * HALF, HDIM), w_ref[1])
        pred_buf[pl.ds(i * PIECES, PIECES)] = pred.astype(BF16).reshape(PIECES, HALF, 2 * FEAT)
        send(i, 0, p_buf, p_out, ROWS)

    def sent(i):
        send(i, 1, pred_buf, pred_out, PIECES)
        send(i, 2, a_buf, a_out, ROWS)
        send(i, 3, r_buf, r_out, ROWS)

    scores, inverses = {0: scored(0)}, {}
    for i in range(STEPS + 2):
        if i + 1 < STEPS:
            scores[i + 1] = scored(i + 1)
        if i < STEPS:
            inverses[i] = softmaxed(i, scores.pop(i))
        if 1 <= i <= STEPS:
            finished(i - 1, inverses.pop(i - 1))
        if i >= 2:
            sent(i - 2)
    for copy in copies:
        copy.wait()


RESIDENT = pl.BlockSpec(memory_space=pltpu.VMEM)
STAYS = pl.BlockSpec(memory_space=pltpu.HBM)


def forward(got, weights):
    *kept, pred = pl.pallas_call(
        forward_kernel,
        in_specs=[RESIDENT, RESIDENT],
        out_specs=[STAYS] * 4,
        out_shape=[
            pltpu.HBM((SEQ, SEQ), BF16),
            pltpu.HBM((SEQ, HDIM), BF16),
            pltpu.HBM((SEQ, HDIM), F32),
            jax.ShapeDtypeStruct((RANKS, HALF, 2 * FEAT), BF16),
        ],
        scratch_shapes=[
            pltpu.VMEM((SEQ, SEQ), BF16),
            pltpu.VMEM((SEQ, HDIM), BF16),
            pltpu.VMEM((SEQ, HDIM), F32),
            pltpu.VMEM((RANKS, HALF, 2 * FEAT), BF16),
            pltpu.SemaphoreType.DMA((4, STEPS)),
        ],
        compiler_params=pltpu.CompilerParams(vmem_limit_bytes=40 << 20),
        cost_estimate=pl.CostEstimate(
            flops=4 * SEQ * SEQ * HDIM, bytes_accessed=12 << 20, transcendentals=SEQ * SEQ
        ),
        name="forward",
    )(got, weights)
    return [pltpu.with_memory_space_constraint(x, pltpu.HBM) for x in kept], pred


def errors_kernel(part_ref, first_ref, second_ref, out_ref):
    total = jnp.concatenate([first_ref[...], second_ref[...]], axis=0)
    for head in range(HEADS):
        total = total + part_ref[head].astype(F32)
    errors = total.astype(BF16)
    for head in range(HEADS):
        out_ref[head] = errors


def make_errors(parts, first, second):
    return pl.pallas_call(
        errors_kernel,
        out_shape=jax.ShapeDtypeStruct((HEADS, TOK, 2 * FEAT), BF16),
        compiler_params=pltpu.CompilerParams(vmem_limit_bytes=8 << 20),
        name="errors",
    )(parts, first, second)


def back_spec(width):
    return pl.BlockSpec((BACK_ROWS, width), lambda i: (i, 0))


def back_packed():
    return pl.BlockSpec((BACK_PIECES, HALF, 2 * FEAT), lambda i: (i, 0, 0))


def backward_kernel(got_ref, w_ref, p_ref, a_ref, r_ref, e_ref, out_ref, gw_ref, dk_acc, dv_acc, gs):
    step = pl.program_id(0)

    @pl.when(step == 0)
    def _():
        dk_acc[...] = jnp.zeros_like(dk_acc)
        dv_acc[...] = jnp.zeros_like(dv_acc)
        gw_ref[...] = jnp.zeros_like(gw_ref)

    q = got_ref[pl.ds(step * BACK_PIECES, BACK_PIECES), 0].reshape(BACK_ROWS, HDIM)
    k = got_ref[:, 1].reshape(SEQ, HDIM)
    v = got_ref[:, 2].reshape(SEQ, HDIM)
    errors = e_ref[...].reshape(BACK_PIECES * HALF, 2 * FEAT)
    first = mm(errors, w_ref[0], NT).reshape(BACK_PIECES, 1, HALF, HDIM)
    second = mm(errors, w_ref[1], NT).reshape(BACK_PIECES, 1, HALF, HDIM)
    grad = jnp.concatenate([first, second], axis=1).reshape(BACK_ROWS, HDIM) * r_ref[...]
    grad = grad.astype(BF16)
    attended = a_ref[...]
    dots = jnp.sum(grad.astype(F32) * attended.astype(F32), axis=-1, keepdims=True)

    def part(i):
        return slice(i * SUB_BACK, (i + 1) * SUB_BACK)

    def scored(i):
        return mm(grad[part(i)], v, NT)

    def weighted(i, grad_probs):
        out = (p_ref[part(i)].astype(F32) * (grad_probs - dots[part(i)])).astype(BF16)
        gs[part(i)] = out
        return out

    def finished(i, grad_scores):
        count = SUB_BACK // TOK
        dq = (mm(grad_scores, k) * SCALE).astype(BF16)
        out_ref[pl.ds(step * BACK_PIECES + i * count, count), 0] = dq.reshape(count, TOK, HDIM)

    subs = BACK_ROWS // SUB_BACK
    grad_probs, grad_scores = {0: scored(0)}, {}
    for i in range(subs + 1):
        if i + 1 < subs:
            grad_probs[i + 1] = scored(i + 1)
        if i < subs:
            grad_scores[i] = weighted(i, grad_probs.pop(i))
        if i >= 1:
            finished(i - 1, grad_scores.pop(i - 1))

    dv_acc[...] += mm(grad, p_ref[...], TN)
    dk_acc[...] += mm(q, gs[...], TN)
    pieces = attended.reshape(BACK_PIECES, 2, HALF, HDIM)
    lane = lax.broadcasted_iota(jnp.int32, (HDIM, 2 * FEAT), 1)
    low = mm(pieces[:, 0].reshape(BACK_PIECES * HALF, HDIM), errors, TN)
    high = mm(pieces[:, 1].reshape(BACK_PIECES * HALF, HDIM), errors, TN)
    gw_ref[...] += jnp.where(lane < FEAT, low, high)

    @pl.when(step == pl.num_programs(0) - 1)
    def _():
        out_ref[:, 1] = (dk_acc[...] * SCALE).astype(BF16).T.reshape(RANKS, TOK, HDIM)
        out_ref[:, 2] = dv_acc[...].astype(BF16).T.reshape(RANKS, TOK, HDIM)


def backward(got, weights, probs, attended, inverse, errors):
    return pl.pallas_call(
        backward_kernel,
        grid=(BACK_STEPS,),
        in_specs=[RESIDENT, RESIDENT, back_spec(SEQ), back_spec(HDIM), back_spec(HDIM), back_packed()],
        out_specs=[
            pl.BlockSpec((RANKS, 3, TOK, HDIM), lambda i: (0, 0, 0, 0)),
            pl.BlockSpec((HDIM, 2 * FEAT), lambda i: (0, 0)),
        ],
        out_shape=[
            jax.ShapeDtypeStruct((RANKS, 3, TOK, HDIM), BF16),
            jax.ShapeDtypeStruct((HDIM, 2 * FEAT), F32),
        ],
        scratch_shapes=[
            pltpu.VMEM((HDIM, SEQ), F32),
            pltpu.VMEM((HDIM, SEQ), F32),
            pltpu.VMEM((BACK_ROWS, SEQ), BF16),
        ],
        compiler_params=pltpu.CompilerParams(vmem_limit_bytes=40 << 20),
        cost_estimate=pl.CostEstimate(
            flops=8 * SEQ * SEQ * HDIM, bytes_accessed=14 << 20, transcendentals=0
        ),
        name="backward",
    )(got, weights, probs, attended, inverse, errors)


CLIP_RANKS = [list(range(clip, RANKS, 2)) for clip in range(2)]
PARTNER = [(i, i ^ 1) for i in range(RANKS)]


def exchange(x, groups=None):
    return lax.all_to_all(
        x, "seq", split_axis=0, concat_axis=0, axis_index_groups=groups, tiled=True
    )


def permute(x, pairs, axis="seq"):
    return lax.ppermute(x, axis, pairs)


def shards(
    frame_features,
    conv_weight,
    conv_bias,
    vae_noise,
    flow_noise,
    head_queries,
    head_keys,
    head_values,
    out_weight,
    out_bias,
):
    rank = lax.axis_index("seq")
    got = exchange(pack(head_queries, head_keys, head_values))

    own, to_next, to_prev = conv(
        frame_features.reshape(512, 512), conv_weight.transpose(0, 2, 1).reshape(864, 512)
    )
    up = [(i, i + 1) for i in range(RANKS - 1)]
    down = [(i + 1, i) for i in range(RANKS - 1)]
    halo = [lax.ppermute(to_next, "seq", up), lax.ppermute(to_prev, "seq", down)]

    head, clip = rank // 2, rank % 2
    head_weight = lax.dynamic_slice(out_weight, (head * HDIM, 0), (HDIM, FEAT))
    empty = jnp.zeros_like(head_weight)
    weights = jnp.stack(
        [
            jnp.concatenate([head_weight, empty], axis=1),
            jnp.concatenate([empty, head_weight], axis=1),
        ]
    )
    (probs, attended, inverse), pred = forward(got, weights)
    attended, own, halo = lax.optimization_barrier((attended, own, halo))
    encoded = own + halo[0] + halo[1]
    encoded = encoded + conv_bias[:, None]
    encoded = encoded.reshape(2, LATC, 2, 4, 2, 16, 2).transpose(0, 2, 3, 5, 1, 4, 6)
    mean_tokens, logvar_tokens = encoded.reshape(2, 2, TOK, FEAT)
    latent = mean_tokens + jnp.exp(0.5 * logvar_tokens) * vae_noise
    base = out_bias - (flow_noise - latent_factor * latent)
    base = base.reshape(2, 2, HALF, FEAT).transpose(0, 2, 1, 3).reshape(2, HALF, 2 * FEAT)
    mine = lax.dynamic_index_in_dim(base, clip, 0, False)
    theirs = permute(lax.dynamic_index_in_dim(base, 1 - clip, 0, False), PARTNER)
    first = jnp.where(clip == 0, mine, theirs)
    second = jnp.where(clip == 0, theirs, mine)

    parts = exchange(pred.reshape(HEADS, TOK, 2 * FEAT), CLIP_RANKS)
    errors = exchange(make_errors(parts, first, second), CLIP_RANKS)
    errors = errors.reshape(RANKS, HALF, 2 * FEAT)
    grads, weight_grad = backward(got, weights, probs, attended, inverse, errors)
    grad_queries, grad_keys, grad_values = unpack(exchange(grads))

    weight_grad = (weight_grad[:, :FEAT] + weight_grad[:, FEAT:]).reshape(2, FEAT, FEAT)
    mine = lax.dynamic_index_in_dim(weight_grad, clip, 0, False)
    theirs = lax.dynamic_index_in_dim(weight_grad, 1 - clip, 0, False)
    total = mine + permute(theirs, PARTNER)
    for bit in (1, 2, 4, 8):
        total = total + permute(total, [(i, i ^ bit) for i in range(16)], "dp")
    return (grad_queries, grad_keys, grad_values, total)


def solution(mesh):
    return jax.shard_map(
        shards,
        mesh=mesh,
        in_specs=(
            P("dp", None, "seq", None, None),
            P(),
            P(),
            P("dp", "seq", None),
            P("dp", "seq", None),
            P("dp", "seq", None),
            P("dp", "seq", None),
            P("dp", "seq", None),
            P(),
            P(),
        ),
        out_specs=(
            P("dp", "seq", None),
            P("dp", "seq", None),
            P("dp", "seq", None),
            P("seq", None),
        ),
        check_vma=False,
    )
```
